32 devices in a mesh: ctx: 16 (over z, x, core), mp: 2 (over y).
Axes of the slice: x: 2, y: 2, z: 4, core: 2. Of those that a mesh axis runs over, the one named last changes fastest.
Arguments:
- query_proj: bfloat16 [2048, 4096], P(('ctx', 'mp')), may hold values from -91.92388 to 91.92388
- keyval_proj: bfloat16 [2048, 8, 256], P(('ctx', 'mp')), may hold values from -12 to 12
- hidden: bfloat16 [2048, 4096], P('ctx', 'mp'), may hold values from -6 to 6
- weight_x: bfloat16 [4096, 1024], P(None, 'mp'), may hold values from -0.09375 to 0.09375
- conv_x: float32 [4, 1024], P(None, 'mp'), may hold values from -3 to 3
- conv_b: float32 [4, 1024], P(None, 'mp'), may hold values from -3 to 3
- conv_c: float32 [4, 4096], P(None, 'mp'), may hold values from -3 to 3
- step_size: float32 [2048, 32], P('ctx', 'mp'), may hold values from 0 to 1.2, as said below
- decay_log: float32 [32], P('mp'), may hold values from -0.5 to 0.5
- skip_gain: float32 [32], P('mp'), may hold values from 0.5 to 1.5
Outputs:
- student_out: bfloat16 [2048, 4096], P('ctx', 'mp')
- weight_grad: float32 [4096, 1024], P('ctx', 'mp')
The draws below stay inside these ranges and needn't reach their ends.
Inputs may be any that keep to these rules, and one draw needn't show every extreme that they name: `step_size`: positive.
All inputs are finite; a program needn't handle non-finite values.
Results may differ from the reference program's by a relative error of at most 0.001.
The reference program's roundings to bfloat16 on the way (of `x_input` and `input_grad`) count: a program that leaves them out, or rounds other values in their place, can miss the bound.
Values may be sent and summed in bfloat16 or wider, within the bound.
No kernel may reach another device: no remote copies, remote signals or barrier semaphores. Data moves between devices by JAX's collectives and lax.ppermute only.
A program may use at most 128 MiB of HBM per device.

```python
import jax
import jax.numpy as jnp
from jax import lax

D = 4096
HEAD_TOTAL = 32
KV = 8
HD = 128
CONV = 4
TOK_DEV = 128
TOKEN_TOTAL = 2048


def draw_query_proj(key, part):
    base_key = jax.random.fold_in(key, 1)
    values = 4.0 * jnp.clip(jax.random.normal(base_key, (TOKEN_TOTAL, HEAD_TOTAL * HD), jnp.float32), -4.0, 4.0)
    return values.astype(jnp.bfloat16)


def draw_keyval_proj(key, part):
    base_key = jax.random.fold_in(key, 2)
    lanes = jnp.arange(2 * HD) < HD
    values = jnp.clip(jax.random.normal(base_key, (TOKEN_TOTAL, KV, 2 * HD), jnp.float32), -4.0, 4.0)
    values = jnp.where(lanes[None, None, :], values, 3.0 * values)
    return values.astype(jnp.bfloat16)


def draw_step_size(key, part):
    kind_key = jax.random.fold_in(key, 21)
    fast_key = jax.random.fold_in(key, 22)
    slow_key = jax.random.fold_in(key, 23)
    rough_key = jax.random.fold_in(key, 24)
    place_key = jax.random.fold_in(key, 25)
    spike_key = jax.random.fold_in(key, 26)
    fast = jax.random.uniform(kind_key, (HEAD_TOTAL,)) < 0.5
    fast_rate = jnp.exp(jax.random.uniform(fast_key, (HEAD_TOTAL,), jnp.float32, jnp.log(1.0 / 50.0), jnp.log(1.0 / 30.0)))
    slow_rate = jnp.exp(jax.random.uniform(slow_key, (HEAD_TOTAL,), jnp.float32, jnp.log(0.3), 0.0)) / TOKEN_TOTAL
    baseline_rate = jnp.where(fast, fast_rate, slow_rate)
    rough_values = jnp.exp(jax.random.uniform(rough_key, (TOKEN_TOTAL, HEAD_TOTAL), jnp.float32, -0.693, 0.693))
    place_indices = jax.random.randint(place_key, (3,), 0, TOKEN_TOTAL)
    amount_values = jax.random.uniform(spike_key, (3, HEAD_TOTAL), jnp.float32, 0.25, 0.35)
    token_positions = jnp.arange(TOKEN_TOTAL)
    spike_values = jnp.zeros((TOKEN_TOTAL, HEAD_TOTAL), jnp.float32)
    for which_index in range(3):
        spike_values = spike_values + jnp.where((token_positions == place_indices[which_index])[:, None], amount_values[which_index][None, :], 0.0)
    return baseline_rate[None, :] * rough_values + spike_values


def level_of(key, dims, split, low, high):
    def one(dim, blocks):
        steps = jax.random.uniform(jax.random.fold_in(jax.random.fold_in(key, 6), dim), (blocks,), jnp.float32, low / len(split), high / len(split))
        return jnp.repeat(jnp.exp(steps), dims[dim] // blocks).reshape((-1,) + (1,) * (len(dims) - dim - 1))

    factor_of = one(*split[0])
    for cut in split[1:]:
        factor_of = factor_of * one(*cut)
    return factor_of


def bell_draw(stream_key, shape, scale, most, shards=(), held_as=jnp.bfloat16):
    loudness = level_of(stream_key, shape, shards, -0.22, 0.18) if shards else 1.0
    values = jax.random.normal(stream_key, shape, jnp.float32) * scale * loudness
    return jnp.minimum(jnp.maximum(values, -most), most).astype(held_as)


def setup_inputs(seed: int = 0) -> dict:
    arg_keys = jax.random.split(jax.random.key(seed), 11)
    return {
        "query_proj": draw_query_proj(jax.random.fold_in(arg_keys[10], 71), 0),
        "keyval_proj": draw_keyval_proj(jax.random.fold_in(arg_keys[10], 71), 0),
        "hidden": bell_draw(arg_keys[2], (TOKEN_TOTAL, D), 1.0, 6.0, ((0, 16), (1, 2))),
        "weight_x": bell_draw(arg_keys[3], (D, KV * HD), D ** -0.5, 0.09375, ((1, 2),)),
        "conv_x": bell_draw(arg_keys[4], (CONV, KV * HD), CONV ** -0.5, 3.0, ((1, 2),), jnp.float32),
        "conv_b": bell_draw(arg_keys[5], (CONV, KV * HD), CONV ** -0.5, 3.0, ((1, 2),), jnp.float32),
        "conv_c": bell_draw(arg_keys[6], (CONV, HEAD_TOTAL * HD), CONV ** -0.5, 3.0, ((1, 2),), jnp.float32),
        "step_size": draw_step_size(jax.random.fold_in(arg_keys[10], 71), 0),
        "decay_log": jnp.clip(jax.random.uniform(arg_keys[8], (HEAD_TOTAL,), jnp.float32, -0.5, 0.5) * level_of(arg_keys[8], (HEAD_TOTAL,), ((0, 2),), -0.4, 0.0), -0.5, 0.5),
        "skip_gain": jnp.clip(0.5 + 1.0 * jax.random.uniform(arg_keys[9], (HEAD_TOTAL,), jnp.float32) ** level_of(arg_keys[9], (HEAD_TOTAL,), ((0, 2),), -0.2, 0.2), 0.5, 1.5),
    }


highest_precision = lax.Precision.HIGHEST

def causal_conv(signal, kernel):
    length = signal.shape[0]
    padded = jnp.pad(signal, ((CONV - 1, 0), (0, 0)))
    result = jnp.zeros_like(signal)
    for offset in range(CONV):
        result = result + kernel[offset][None, :] * padded[offset:offset + length]
    return result

def teacher_attention(query_proj, keyval_proj):
    per_group = HEAD_TOTAL // KV
    key_all = keyval_proj[:, :, :HD].astype(jnp.float32)
    value_all = keyval_proj[:, :, HD:].astype(jnp.float32)
    queries = query_proj.reshape(TOKEN_TOTAL, KV, per_group, HD)
    block_size = TOK_DEV
    block_count = TOKEN_TOTAL // block_size
    token_positions = jnp.arange(TOKEN_TOTAL, dtype=jnp.int32)

    def per_block(block_index):
        first = block_index * block_size
        query_block = lax.dynamic_slice_in_dim(queries, first, block_size, 0)
        row_pos = first + jnp.arange(block_size, dtype=jnp.int32)
        allowed = token_positions[None, :] <= row_pos[:, None]

        def per_head_group(group_index):
            query_group = lax.dynamic_index_in_dim(query_block, group_index, 1, keepdims=False).astype(jnp.float32)
            key_group = lax.dynamic_index_in_dim(key_all, group_index, 1, keepdims=False)
            value_group = lax.dynamic_index_in_dim(value_all, group_index, 1, keepdims=False)
            scores = jnp.einsum('brd,kd->rbk', query_group, key_group) * HD ** (-0.5)
            scores = jnp.where(allowed[None], scores, -1e+30)
            row_max = lax.optimization_barrier(jnp.max(scores, axis=2, keepdims=True))
            weights = jnp.where(allowed[None], jnp.exp(scores - row_max), 0.0)
            totals = lax.optimization_barrier(jnp.sum(weights, axis=2, keepdims=True))
            rounded = lax.optimization_barrier(weights.astype(jnp.bfloat16)).astype(jnp.float32)
            mixed = jnp.einsum('rbk,kd->rbd', rounded, value_group)
            return jnp.transpose(mixed / totals, (1, 0, 2))
        return lax.map(per_head_group, jnp.arange(KV, dtype=jnp.int32))
    blocks = lax.map(per_block, jnp.arange(block_count, dtype=jnp.int32))
    return jnp.transpose(blocks, (0, 2, 1, 3, 4)).reshape(TOKEN_TOTAL, HEAD_TOTAL * HD)

def student_scan(x_conv, b_conv, c_conv, step_size, decay_log, skip_gain):
    per_group = HEAD_TOTAL // KV
    block_size = TOK_DEV
    block_count = TOKEN_TOTAL // block_size
    decay_rate = -jnp.exp(decay_log).reshape(KV, per_group)
    skip_heads = skip_gain.reshape(KV, per_group)
    x_blocks = x_conv.reshape(block_count, block_size, KV, HD)
    b_blocks = b_conv.reshape(block_count, block_size, KV, HD)
    c_blocks = c_conv.reshape(block_count, block_size, KV, per_group, HD)
    step_blocks = step_size.reshape(block_count, block_size, KV, per_group)
    causal = jnp.arange(block_size)[:, None] >= jnp.arange(block_size)[None, :]

    def advance(state_now, inputs):
        x_block, input_proj_block, readout_block, step_block = inputs
        log_decay = jnp.cumsum(step_block * decay_rate[None], axis=0)
        ordered = jnp.transpose(log_decay, (1, 2, 0))
        differ = ordered[:, :, :, None] - ordered[:, :, None, :]
        within = jnp.where(causal, jnp.exp(jnp.where(causal, differ, 0.0)), 0.0)
        pairwise_scores = jnp.einsum('qmzo,imo->mzqi', readout_block, input_proj_block, precision=highest_precision)
        mixing_weights = pairwise_scores * within
        driven_state = step_block[..., None] * x_block[:, :, None, :]
        inner_portion = jnp.einsum('hewl,lhen->when', mixing_weights, driven_state, precision=highest_precision)
        carried = jnp.exp(log_decay)[..., None] * jnp.einsum('tgrn,grnp->tgrp', readout_block, state_now, precision=highest_precision)
        output = inner_portion + carried + skip_heads[None, :, :, None] * x_block[:, :, None, :]
        to_end = jnp.exp(log_decay[-1][None] - log_decay)
        added = jnp.einsum('sgn,sgrp->grnp', input_proj_block, to_end[..., None] * driven_state, precision=highest_precision)
        state_next = jnp.exp(log_decay[-1])[..., None, None] * state_now + added
        return (state_next, output)
    start_state = jnp.zeros((KV, per_group, HD, HD), jnp.float32)
    final_state, outputs = lax.scan(advance, start_state, (x_blocks, b_blocks, c_blocks, step_blocks))
    return outputs.reshape(TOKEN_TOTAL, HEAD_TOTAL * HD)

def reference(query_proj, keyval_proj, hidden, weight_x, conv_x, conv_b, conv_c, step_size, decay_log, skip_gain):
    x_input = jnp.dot(hidden, weight_x, preferred_element_type=jnp.float32).astype(jnp.bfloat16)
    x_pre = causal_conv(x_input.astype(jnp.float32), conv_x)
    x_conv = jax.nn.silu(x_pre)
    key_rows = keyval_proj[:, :, :HD].reshape(TOKEN_TOTAL, KV * HD).astype(jnp.float32)
    b_conv = jax.nn.silu(causal_conv(key_rows, conv_b))
    c_conv = jax.nn.silu(causal_conv(query_proj.astype(jnp.float32), conv_c))

    def forward(value):
        return student_scan(value, b_conv, c_conv, step_size, decay_log, skip_gain)
    student, pullback = jax.vjp(forward, x_conv)
    target = teacher_attention(query_proj, keyval_proj)
    upstream_gradient = 2.0 * (student - target) / (HEAD_TOTAL * HD)
    x_grad = pullback(upstream_gradient)[0]
    sigmoid_x = jax.nn.sigmoid(x_pre)
    pre_grad = x_grad * sigmoid_x * (1.0 + x_pre * (1.0 - sigmoid_x))
    padded = jnp.pad(pre_grad, ((0, CONV - 1), (0, 0)))
    input_grad = jnp.zeros_like(pre_grad)
    for offset in range(CONV):
        input_grad = input_grad + conv_x[offset][None, :] * padded[CONV - 1 - offset:CONV - 1 - offset + TOKEN_TOTAL]
    weight_grad = jnp.dot(hidden.T, input_grad.astype(jnp.bfloat16), preferred_element_type=jnp.float32)
    return (student.astype(jnp.bfloat16), weight_grad)
```

```python
import jax
import jax.numpy as jnp
from jax import lax
from jax.experimental import pallas as pl
from jax.experimental.pallas import tpu as pltpu
from jax.sharding import Mesh
from jax.sharding import PartitionSpec as P

HEAD_TOTAL = 32
KV = 8
HD = 128
CONV = 4


highest_precision = lax.Precision.HIGHEST
negative = -1e30


def shifted(value, axis, steps):
    count = lax.axis_size(axis)
    leading, last = (max(0, -steps), min(count, count - steps))
    return lax.ppermute(value, axis, [(source, source + steps) for source in range(leading, last)])


def carried_in(value, axis, join, neutral, backward):
    count, mine = (lax.axis_size(axis), lax.axis_index(axis))
    pieces = jax.tree.map(lambda part: lax.all_gather(part, axis), value)
    if backward:
        pieces = jax.tree.map(lambda part: part[::-1], pieces)
        mine = count - 1 - mine
    subtotal = jax.tree.map(
        lambda part, zero: jnp.full_like(part, 0) + jnp.asarray(zero, part.dtype), value, neutral
    )

    def lap(position, subtotal):
        longer = join(subtotal, jax.tree.map(lambda part: part[position], pieces))
        return jax.tree.map(lambda new, old: jnp.where(position < mine, new, old), longer, subtotal)

    return lax.fori_loop(0, count - 1, lap, subtotal)


def causal_conv(head_rows, signal, kernel):
    length = signal.shape[0]
    extended = jnp.concatenate([head_rows, signal], axis=0).astype(jnp.float32)
    result = jnp.zeros((length, signal.shape[1]), jnp.float32)
    for offset in range(CONV):
        result = result + kernel[offset][None, :] * extended[offset : offset + length]
    return result


def chain_combine(earlier, later):
    return (earlier[0] * later[0], later[0][..., None, None] * earlier[1] + later[1])


def sequence_local(
    query_proj,
    keyval_proj,
    hidden,
    weight_x,
    conv_x,
    conv_b,
    conv_c,
    step_size,
    decay_log,
    skip_gain,
):
    groups = KV // lax.axis_size("mp")
    per_group = HEAD_TOTAL // KV
    group_width = per_group * HD
    raw_count = query_proj.shape[0]
    query_grouped = query_proj.reshape(raw_count, KV, group_width)
    query_local, keyval_local = (
        lax.all_to_all(query_grouped, "mp", split_axis=1, concat_axis=0, tiled=True),
        lax.all_to_all(keyval_proj, "mp", split_axis=1, concat_axis=0, tiled=True),
    )
    row_count = query_local.shape[0]
    shard_index = lax.axis_index("ctx")
    first_row = shard_index * row_count
    row_positions = first_row + jnp.arange(row_count, dtype=jnp.int32)
    query_total = per_group * row_count
    query_heads = jnp.transpose(
        query_local.reshape(row_count, groups, per_group, HD), (1, 2, 0, 3)
    ).reshape(groups, query_total, HD)
    query_pos = jnp.tile(row_positions, per_group)
    last_query = jnp.max(row_positions)
    score_scale = HD ** (-0.5)

    def attend_all(state_carry, shard_piece):
        piece_rows = shard_piece.shape[0]
        block_size = 512
        block_count = piece_rows // block_size
        blocks = shard_piece.reshape(block_count, block_size, groups, 2 * HD)

        def one_block(inner_carry, block_index):
            row_max, norm_total, weighted = inner_carry
            key_block = lax.dynamic_index_in_dim(blocks, block_index, 0, keepdims=False)
            scores = (
                jnp.einsum(
                    "gqd,kgd->gqk",
                    query_heads,
                    key_block[:, :, :HD],
                    preferred_element_type=jnp.float32,
                )
                * score_scale
            )
            key_pos = block_index * block_size + jnp.arange(block_size, dtype=jnp.int32)
            allowed = (key_pos[None, :] <= query_pos[:, None])[None]
            scores = jnp.where(allowed, scores, negative)
            new_max = jnp.maximum(row_max, jnp.max(scores, axis=2))
            weights = jnp.where(allowed, jnp.exp(scores - new_max[:, :, None]), 0.0)
            factor = jnp.exp(row_max - new_max)
            norm_total = norm_total * factor + jnp.sum(weights, axis=2)
            mixed = jnp.einsum(
                "gqk,kgd->gqd",
                weights.astype(jnp.bfloat16),
                key_block[:, :, HD:],
                preferred_element_type=jnp.float32,
            )
            weighted = weighted * factor[:, :, None] + mixed
            return ((new_max, norm_total, weighted), None)

        result, unused = lax.scan(one_block, state_carry, jnp.arange(block_count, dtype=jnp.int32))
        return result

    start_carry = (
        jnp.full((groups, query_total), negative, jnp.float32),
        jnp.zeros((groups, query_total), jnp.float32),
        jnp.zeros((groups, query_total, HD), jnp.float32),
    )
    shard_piece = lax.all_gather(keyval_local, "ctx", axis=0, tiled=True)
    row_max, norm_total, weighted = lax.cond(
        jnp.int32(0) > last_query,
        lambda kept: kept,
        lambda kept: attend_all(kept, shard_piece),
        start_carry,
    )
    target = jnp.transpose(
        (weighted / norm_total[..., None]).reshape(groups, per_group, row_count, HD), (2, 0, 1, 3)
    )
    x_input = jnp.dot(
        lax.all_gather(hidden, "mp", axis=1, tiled=True),
        weight_x,
        preferred_element_type=jnp.float32,
    ).astype(jnp.bfloat16)
    rim_width = CONV - 1
    x_width = groups * HD
    key_rows = keyval_local[:, :, :HD].reshape(row_count, x_width)
    query_rows = query_local.reshape(row_count, groups * group_width)
    tail_rows = jnp.concatenate(
        [x_input[-rim_width:], key_rows[-rim_width:], query_rows[-rim_width:]], axis=1
    )
    before = shifted(tail_rows, "ctx", 1)
    x_pre = causal_conv(before[:, :x_width], x_input, conv_x)
    x_conv = jax.nn.silu(x_pre)
    b_conv = jax.nn.silu(causal_conv(before[:, x_width : 2 * x_width], key_rows, conv_b))
    c_conv = jax.nn.silu(causal_conv(before[:, 2 * x_width :], query_rows, conv_c))
    x_groups = x_conv.reshape(row_count, groups, HD)
    input_proj_groups = b_conv.reshape(row_count, groups, HD)
    readout_heads = c_conv.reshape(row_count, groups, per_group, HD)
    step_heads = step_size.reshape(row_count, groups, per_group)
    decay_rate = -jnp.exp(decay_log).reshape(groups, per_group)
    skip_heads = skip_gain.reshape(groups, per_group)
    log_decay = jnp.cumsum(step_heads * decay_rate[None], axis=0)
    ordered = jnp.transpose(log_decay, (1, 2, 0))
    causal = jnp.arange(row_count)[:, None] >= jnp.arange(row_count)[None, :]
    differ = ordered[:, :, :, None] - ordered[:, :, None, :]
    within = jnp.where(causal, jnp.exp(jnp.where(causal, differ, 0.0)), 0.0)
    pairwise_scores = jnp.einsum(
        "qmzo,imo->mzqi", readout_heads, input_proj_groups, precision=highest_precision
    )
    mixing_weights = pairwise_scores * within
    driven_state = step_heads[..., None] * x_groups[:, :, None, :]
    inner_portion = jnp.einsum(
        "hewl,lhen->when", mixing_weights, driven_state, precision=highest_precision
    )
    to_end = jnp.exp(log_decay[-1][None] - log_decay)
    local_state = jnp.einsum(
        "sgn,sgrp->grnp",
        input_proj_groups,
        to_end[..., None] * driven_state,
        precision=highest_precision,
    )
    block_decay = jnp.exp(log_decay[-1])
    identity = (jnp.ones_like(block_decay), jnp.zeros_like(local_state))
    chained = carried_in((block_decay, local_state), "ctx", chain_combine, identity, False)
    incoming = chained[1]
    growth = jnp.exp(log_decay)
    carried = growth[..., None] * jnp.einsum(
        "tgrn,grnp->tgrp", readout_heads, incoming, precision=highest_precision
    )
    student = inner_portion + carried + skip_heads[None, :, :, None] * x_groups[:, :, None, :]
    upstream_gradient = 2.0 * (student - target) / (HEAD_TOTAL * HD)
    state_grad = jnp.einsum(
        "tgrn,tgrp->grnp",
        growth[..., None] * readout_heads,
        upstream_gradient,
        precision=highest_precision,
    )
    reverse = carried_in((block_decay, state_grad), "ctx", chain_combine, identity, True)
    later_grad = reverse[1]
    inner_backward = jnp.einsum(
        "lvyq,ylve->qlve", mixing_weights, upstream_gradient, precision=highest_precision
    )
    back_state = to_end[..., None] * jnp.einsum(
        "sgn,grnp->sgrp", input_proj_groups, later_grad, precision=highest_precision
    )
    head_grad = (
        step_heads[..., None] * (inner_backward + back_state)
        + skip_heads[None, :, :, None] * upstream_gradient
    )
    x_grad = jnp.sum(head_grad, axis=2).reshape(row_count, x_width)
    sigmoid_x = jax.nn.sigmoid(x_pre)
    pre_grad = x_grad * sigmoid_x * (1.0 + x_pre * (1.0 - sigmoid_x))
    after = shifted(pre_grad[:rim_width], "ctx", -1)
    extended = jnp.concatenate([pre_grad, after], axis=0)
    input_grad = jnp.zeros_like(pre_grad)
    for offset in range(CONV):
        input_grad = (
            input_grad
            + conv_x[offset][None, :] * extended[CONV - 1 - offset : CONV - 1 - offset + row_count]
        )
    input_rounded = input_grad.astype(jnp.bfloat16)
    hidden_whole = lax.all_gather(hidden, "mp", axis=1, tiled=True)
    weight_grad = lax.psum_scatter(
        lax.dot_general(
            hidden_whole,
            input_rounded,
            (((0,), (0,)), ((), ())),
            preferred_element_type=jnp.float32,
        ),
        "ctx",
        scatter_dimension=0,
        tiled=True,
    )
    student_out = student.reshape(row_count, groups * group_width).astype(jnp.bfloat16)
    return (student_out, weight_grad)


CHUNK = 256
SWAP = ((0, 1), (1, 0))
bf16, f32 = jnp.bfloat16, jnp.float32
NT = (((1,), (1,)), ((), ()))
TN = (((0,), (0,)), ((), ()))
NN = (((1,), (0,)), ((), ()))
VMEM_BLOCK = pl.BlockSpec(memory_space=pltpu.VMEM)
SMEM_BLOCK = pl.BlockSpec(memory_space=pltpu.SMEM)
PARAMS = pltpu.CompilerParams(vmem_limit_bytes=56 * 1024 * 1024)


def swap(value, axis):
    return lax.ppermute(value, axis, SWAP)


def split(value):
    high = value.astype(bf16)
    return high, (value - high.astype(f32)).astype(bf16)


def dot3(left, right, dims):
    (left_axis,), (right_axis,) = dims[0]
    lh, ll = split(left)
    rh, rl = split(right)
    return lax.dot_general(
        jnp.concatenate([lh, ll, lh], axis=left_axis),
        jnp.concatenate([rh, rh, rl], axis=right_axis),
        dims,
        preferred_element_type=f32,
    )


def rows(index, size):
    return pl.ds(pl.multiple_of(index * size, size), size)


def attend_kernel(where_ref, q_ref, *refs):
    kv_refs, (out_ref, kv_all) = refs[:4], refs[4:]
    tokens = q_ref.shape[0]
    place = where_ref[1]
    block = tokens // 16
    for delta in range(4):
        for z in range(4):
            kv_all[rows(z * 4 + (place ^ delta), block), :] = kv_refs[delta][z * block : (z + 1) * block, :]
    scale = HD ** (-0.5)
    diag = lax.broadcasted_iota(jnp.int32, (CHUNK, CHUNK), 0) >= lax.broadcasted_iota(
        jnp.int32, (CHUNK, CHUNK), 1
    )
    for i in range(tokens // CHUNK):
        q = q_ref[i * CHUNK : (i + 1) * CHUNK, :]
        last = lax.dot_general(
            q, kv_all[i * CHUNK : (i + 1) * CHUNK, :HD], NT, preferred_element_type=f32
        )
        last = jnp.where(diag, last, negative)
        if i:
            score = lax.dot_general(q, kv_all[: i * CHUNK, :HD], NT, preferred_element_type=f32)
            score = jnp.concatenate([score, last], axis=1)
        else:
            score = last
        top = jnp.max(score, axis=1, keepdims=True)
        weight = jnp.exp((score - top) * scale)
        total = jnp.sum(weight, axis=1, keepdims=True)
        mixed = lax.dot_general(
            weight.astype(bf16), kv_all[: (i + 1) * CHUNK, HD:], NN, preferred_element_type=f32
        )
        out_ref[i * CHUNK : (i + 1) * CHUNK, :] = mixed / total


def silu(value):
    return value / (1.0 + jnp.exp(-value))


def student_kernel(where_ref, rate_ref, skip_ref, q_ref, target_ref, conv_x_ref, conv_b_ref, conv_c_ref, *refs):
    kv_refs, x_refs = refs[:4], refs[4:8]
    y_ref, grad_ref = refs[8:10]
    x_pad, b_pad, c_pad, b_all, c_all, slope_all, y_all, dt_all = refs[10:]
    tokens = q_ref.shape[0]
    count = tokens // CHUNK
    block = tokens // 16
    z_mine, place, head = where_ref[0], where_ref[1], where_ref[2]
    rim = 8
    for pad in (x_pad, b_pad, c_pad):
        pad[0:rim, :] = jnp.zeros((rim, HD), f32)
    mine = lax.broadcasted_iota(jnp.int32, (16, HD), 0) % 4 == place
    for delta in range(4):
        for z in range(4):
            index = z * 4 + (place ^ delta)
            at = pl.ds(pl.multiple_of(rim + index * block, 8), block)
            x_pad[at, :] = x_refs[delta][z, :block, :].astype(f32)
            b_pad[at, :] = kv_refs[delta][z * block : (z + 1) * block, :HD].astype(f32)
            pieces = x_refs[delta][z, block : block + 16, :].astype(f32)
            step = jnp.sum(jnp.where(mine, pieces, 0.0), axis=0, keepdims=True)
            dt_all[rows(index, 8), :] = jnp.broadcast_to(step, (8, HD))
    c_pad[rim : rim + tokens, :] = q_ref[...].astype(f32)
    taps_x = conv_x_ref[:, pl.ds(pl.multiple_of(z_mine * HD, HD), HD)]
    taps_b = conv_b_ref[:, pl.ds(pl.multiple_of(z_mine * HD, HD), HD)]
    taps_c = conv_c_ref[:, pl.ds(pl.multiple_of(head * HD, HD), HD)]
    rate = -jnp.exp(jnp.full((1, HD), rate_ref[head], f32))[:, :1]
    skip = skip_ref[head]
    row_id = lax.broadcasted_iota(jnp.int32, (CHUNK, CHUNK), 0)
    col_id = lax.broadcasted_iota(jnp.int32, (CHUNK, CHUNK), 1)

    def conv(pad, taps, i):
        piece = pad[pl.ds(pl.multiple_of(i * CHUNK, CHUNK), CHUNK + rim), :]
        result = taps[0:1, :] * piece[rim - 3 : rim - 3 + CHUNK, :]
        for offset in range(1, CONV):
            result = result + taps[offset : offset + 1, :] * piece[rim - 3 + offset : rim - 3 + offset + CHUNK, :]
        return result

    def decays(i):
        step_row = jnp.concatenate(
            [dt_all[rows(i * 2, 8), :][0:1, :], dt_all[rows(i * 2 + 1, 8), :][0:1, :]], axis=1
        )
        wide = jnp.broadcast_to(step_row, (CHUNK, CHUNK))
        step_col = jnp.sum(jnp.where(row_id == col_id, wide, 0.0), axis=1, keepdims=True)
        cum_col = jnp.sum(jnp.where(col_id <= row_id, wide, 0.0), axis=1, keepdims=True) * rate
        cum_row = jnp.sum(jnp.where(row_id <= col_id, step_col, 0.0), axis=0, keepdims=True) * rate
        end = cum_row[:, CHUNK - 1 :]
        return step_row, step_col, cum_row, cum_col, end

    def forward(i, state):
        at = rows(i, CHUNK)
        x_pre = conv(x_pad, taps_x, i)
        gate = 1.0 / (1.0 + jnp.exp(-x_pre))
        x = x_pre * gate
        slope_all[at, :] = gate * (1.0 + x_pre * (1.0 - gate))
        b = silu(conv(b_pad, taps_b, i))
        c = silu(conv(c_pad, taps_c, i))
        step_row, step_col, cum_row, cum_col, end = decays(i)
        within = jnp.exp(jnp.where(row_id >= col_id, cum_col - cum_row, negative))
        mix = dot3(c, b, NT) * within * step_row
        grown = c * jnp.exp(cum_col)
        fed = b * (jnp.exp(end - cum_col) * step_col)
        b_all[at, :] = b
        c_all[at, :] = c
        y = dot3(jnp.concatenate([mix, grown], axis=1), jnp.concatenate([x, state], axis=0), NN)
        y = y + skip * x
        y_all[at, :] = y
        y_ref[at, :] = y.astype(bf16)
        return jnp.exp(end) * state + dot3(fed, x, TN)

    lax.fori_loop(0, count, forward, jnp.zeros((HD, HD), f32))

    def backward(k, carry):
        state, later = carry
        i = count - 1 - k
        at = rows(i, CHUNK)
        up = (y_all[at, :] - target_ref[at, :]) * (2.0 / (HEAD_TOTAL * HD))
        b, c = b_all[at, :], c_all[at, :]
        step_row, step_col, cum_row, cum_col, end = decays(i)
        within = jnp.exp(jnp.where(row_id <= col_id, cum_row - cum_col, negative))
        mix = dot3(b, c, NT) * within * step_col
        grown = c * jnp.exp(cum_col)
        fed = b * (jnp.exp(end - cum_col) * step_col)
        dx = dot3(jnp.concatenate([mix, fed], axis=1), jnp.concatenate([up, state], axis=0), NN)
        pre_grad = (dx + skip * up) * slope_all[at, :]
        piece = jnp.concatenate([pre_grad, later], axis=0)
        result = taps_x[0:1, :] * piece[3 : 3 + CHUNK, :]
        for offset in range(1, CONV):
            result = result + taps_x[offset : offset + 1, :] * piece[3 - offset : 3 - offset + CHUNK, :]
        grad_ref[at, :] = result
        return jnp.exp(end) * state + dot3(grown, up, TN), pre_grad[:rim, :]

    lax.fori_loop(0, count, backward, (jnp.zeros((HD, HD), f32), jnp.zeros((rim, HD), f32)))


def weight_kernel(where_ref, h_ref, *refs):
    g_refs, out_ref = refs[:-1], refs[-1]
    z_mine, place = where_ref[0], where_ref[1]
    quarter = h_ref.shape[0] // 4
    for dz in range(4):
        total = jnp.zeros((h_ref.shape[1], HD), f32)
        for de in range(4):
            total = total + lax.dot_general(
                h_ref[rows(place ^ de, quarter), :], g_refs[de][dz], TN, preferred_element_type=f32
            )
        out_ref[:, pl.ds(pl.multiple_of((z_mine ^ dz) * HD, HD), HD)] = total


def head_local(
    query_proj,
    keyval_proj,
    hidden,
    weight_x,
    conv_x,
    conv_b,
    conv_c,
    step_size,
    decay_log,
    skip_gain,
):
    groups = KV // lax.axis_size("mp")
    per_group = HEAD_TOTAL // KV
    heads = groups * per_group
    ctx = ("z", "x", "k")
    z, x, k, m = (lax.axis_index(name) for name in ("z", "x", "k", "mp"))
    place = 2 * x + k
    where = jnp.stack([z, place, z * 4 + place]).astype(jnp.int32)
    raw = query_proj.shape[0]
    block = hidden.shape[0]
    tokens = block * heads
    half = hidden.shape[1]
    mp = lax.axis_size("mp")

    hidden_other = swap(hidden, "mp")
    first = m == 0
    hidden_whole = jnp.concatenate(
        [jnp.where(first, hidden, hidden_other), jnp.where(first, hidden_other, hidden)], axis=1
    )
    q = query_proj.reshape(raw, mp, heads, HD).transpose(2, 1, 0, 3).reshape(mp * heads, raw, HD)
    q = lax.all_to_all(q, ctx + ("mp",), split_axis=0, concat_axis=0, tiled=True).reshape(tokens, HD)
    kv = keyval_proj.reshape(raw, mp, groups, 2 * HD).transpose(2, 1, 0, 3).reshape(KV, raw, 2 * HD)
    kv = lax.all_to_all(kv, ("z", "mp"), split_axis=0, concat_axis=0, tiled=True)
    kv_0 = kv.reshape(KV * raw, 2 * HD)
    kv_2 = swap(kv_0, "x")
    kv_1, kv_3 = swap(kv_0, "k"), swap(kv_2, "k")
    kvs = (kv_0, kv_1, kv_2, kv_3)

    x_input = jnp.dot(hidden_whole, weight_x, preferred_element_type=f32).astype(bf16)
    x_send = x_input.reshape(block, groups, HD).transpose(1, 0, 2)
    step = step_size.T.reshape(groups, 1, per_group, block)
    high = lax.reduce_precision(step, 8, 7)
    middle = lax.reduce_precision(step - high, 8, 7)
    low = step - high - middle
    pieces = jnp.concatenate([high, middle, low, jnp.zeros_like(low)], axis=1)
    pieces = pieces.reshape(groups, 4 * per_group, block).astype(bf16)
    x_send = jnp.concatenate([x_send, pieces], axis=1)
    x_0 = lax.all_to_all(x_send, "z", split_axis=0, concat_axis=0, tiled=True)
    x_2 = swap(x_0, "x")
    x_1, x_3 = swap(x_0, "k"), swap(x_2, "k")
    xs = (x_0, x_1, x_2, x_3)

    h_part = lax.dynamic_slice_in_dim(hidden_whole, m * raw, raw, 0)
    h_part = h_part.reshape(raw, heads, mp * half // heads).transpose(1, 0, 2)
    h_part = lax.all_to_all(h_part, ctx, split_axis=0, concat_axis=0, tiled=True)
    h_other = swap(h_part, "mp")
    h_cols = jnp.stack(
        [jnp.where(first, h_part, h_other), jnp.where(first, h_other, h_part)], axis=1
    ).reshape(tokens, h_part.shape[2])

    target = pl.pallas_call(
        attend_kernel,
        out_shape=jax.ShapeDtypeStruct((tokens, HD), f32),
        in_specs=[SMEM_BLOCK] + [VMEM_BLOCK] * 5,
        out_specs=VMEM_BLOCK,
        scratch_shapes=[pltpu.VMEM((tokens, 2 * HD), bf16)],
        compiler_params=PARAMS,
        cost_estimate=pl.CostEstimate(
            flops=2 * tokens * tokens * HD, transcendentals=tokens * tokens // 2, bytes_accessed=tokens * HD * 12
        ),
        name="attend",
    )(where, q, *kvs)
    scratch = lambda pad=0: pltpu.VMEM((tokens + pad, HD), f32)
    y, grad = pl.pallas_call(
        student_kernel,
        out_shape=(jax.ShapeDtypeStruct((tokens, HD), bf16), jax.ShapeDtypeStruct((tokens, HD), f32)),
        in_specs=[SMEM_BLOCK] * 3 + [VMEM_BLOCK] * 13,
        out_specs=(VMEM_BLOCK, VMEM_BLOCK),
        scratch_shapes=[scratch(8), scratch(8), scratch(8)]
        + [scratch() for _ in range(4)]
        + [pltpu.VMEM((16 * 8, HD), f32)],
        compiler_params=PARAMS,
        cost_estimate=pl.CostEstimate(
            flops=24 * tokens * CHUNK * HD, transcendentals=tokens * CHUNK, bytes_accessed=tokens * HD * 20
        ),
        name="student",
    )(where, decay_log, skip_gain, q, target, conv_x, conv_b, conv_c, *kvs, *xs)

    out = lax.all_to_all(y.reshape(heads, block, HD), ctx, split_axis=0, concat_axis=0, tiled=True)
    student_out = out.transpose(1, 0, 2).reshape(block, heads * HD)

    grad = grad.reshape(2, 2, tokens // 4, HD)
    pick = lambda array, index, axis: lax.dynamic_index_in_dim(array, index, axis, keepdims=False)
    grad = pick(grad, k, 1) + swap(pick(grad, 1 - k, 1), "k")
    grad = pick(grad, x, 0) + swap(pick(grad, 1 - x, 0), "x")
    rounded = grad.astype(bf16)
    spread = [rounded] + [
        lax.ppermute(rounded, "z", [(i, i ^ d) for i in range(groups)]) for d in range(1, groups)
    ]
    g_0 = jnp.stack(spread)
    g_2 = swap(g_0, "x")
    g_1, g_3 = swap(g_0, "k"), swap(g_2, "k")
    weight_grad = pl.pallas_call(
        weight_kernel,
        out_shape=jax.ShapeDtypeStruct((h_cols.shape[1], groups * HD), f32),
        in_specs=[SMEM_BLOCK] + [VMEM_BLOCK] * 5,
        out_specs=VMEM_BLOCK,
        compiler_params=PARAMS,
        name="weight",
    )(where, h_cols, g_0, g_1, g_2, g_3)
    return (student_out, weight_grad)


def solution(mesh):
    ctx, mp = mesh.shape["ctx"], mesh.shape["mp"]
    groups, per_group = KV // mp, HEAD_TOTAL // KV
    by_head = ctx == groups * per_group and per_group == 4 and groups == 4 and mp == 2
    if by_head:
        mesh = Mesh(mesh.devices.reshape(groups, 2, 2, mp), ("z", "x", "k", "mp"))
        local, rows_axes = head_local, ("z", "x", "k")
    else:
        local, rows_axes = sequence_local, ("ctx",)
    both = rows_axes + ("mp",)
    return jax.shard_map(
        local,
        mesh=mesh,
        in_specs=(
            P(both, None),
            P(both, None, None),
            P(rows_axes, "mp"),
            P(None, "mp"),
            P(None, "mp"),
            P(None, "mp"),
            P(None, "mp"),
            P(rows_axes, "mp"),
            P("mp"),
            P("mp"),
        ),
        out_specs=(P(rows_axes, "mp"), P(rows_axes, "mp")),
        check_vma=False,
    )
```
